32 devices in a mesh: grp: 4 (over y, x), rep: 8 (over z, core).
Axes of the slice: x: 2, y: 2, z: 4, core: 2. Of those that a mesh axis runs over, the one named last changes fastest.
Arguments:
- inputs: bfloat16 [8, 512, 768], P('rep', 'grp'), may hold values from -6 to 6
- qkv_weight: bfloat16 [768, 2304], P('grp'), may hold values from -0.21650635 to 0.21650635
- qkv_bias: bfloat16 [2304], P('grp'), may hold values from -3 to 3
- out_weight: bfloat16 [768, 768], P('grp'), may hold values from -0.625 to 0.625
- out_bias: bfloat16 [768], P('grp'), may hold values from -3 to 3
- up_weight: bfloat16 [768, 3072], P('grp'), may hold values from -0.21875 to 0.21875
- up_bias: bfloat16 [3072], P('grp'), may hold values from -3 to 3
- down_weight: bfloat16 [3072, 768], P('grp'), may hold values from -0.109375 to 0.109375
- down_bias: bfloat16 [768], P('grp'), may hold values from -3 to 3
- attn_gain: bfloat16 [768], P('grp'), may hold values from 0.5 to 1.5
- attn_shift: bfloat16 [768], P('grp'), may hold values from -2 to 2
- mlp_gain: bfloat16 [768], P('grp'), may hold values from 0.5 to 1.5
- mlp_shift: bfloat16 [768], P('grp'), may hold values from -2 to 2
- cotangent: float32 [8, 512, 768], P('rep', 'grp'), may hold values from -6 to 6
Outputs:
- block_out: float32 [8, 512, 768], P('rep', 'grp')
- input_grad: float32 [8, 512, 768], P('rep', 'grp')
- qkv_weight_grad: float32 [768, 2304], P('grp')
- qkv_bias_grad: float32 [2304], P('grp')
- out_weight_grad: float32 [768, 768], P('grp')
- out_bias_grad: float32 [768], P('grp')
- up_weight_grad: float32 [768, 3072], P('grp')
- up_bias_grad: float32 [3072], P('grp')
- down_weight_grad: float32 [3072, 768], P('grp')
- down_bias_grad: float32 [768], P('grp')
- attn_gain_grad: float32 [768], P('grp')
- attn_shift_grad: float32 [768], P('grp')
- mlp_gain_grad: float32 [768], P('grp')
- mlp_shift_grad: float32 [768], P('grp')
The draws below stay inside these ranges and needn't reach their ends.
All inputs are finite; a program needn't handle non-finite values.
Results may differ from the reference program's by a relative error of at most 0.0093.
Values may be sent and summed in bfloat16 or wider, within the bound.
A program may use at most 128 MiB of HBM per device.

```python
import jax
import jax.numpy as jnp
from jax import lax

D = 768
HEADS = 12
HD = 64
ROT = 16
FF = 3072
SEQ = 512
SEQS = 8


def draw_inputs(key, part):
    base = jnp.clip(jax.random.normal(jax.random.fold_in(key, 11), (SEQS, SEQ, D), jnp.float32), -6.0, 6.0)
    return base.astype(jnp.bfloat16)


def draw_qkv_weight(key, part):
    base = jnp.clip(jax.random.normal(jax.random.fold_in(key, 21), (D, 3 * D), jnp.float32), -6.0, 6.0) * D ** (-0.5)
    return base.astype(jnp.bfloat16)


def block_scale(own_key, dims, cuts, smallest, top_value):
    level, own = 1.0, jax.random.fold_in(own_key, 6)
    for position, shards_of in cuts:
        heights = jnp.exp(jax.random.uniform(jax.random.fold_in(own, position), (shards_of,), jnp.float32, smallest / len(cuts), top_value / len(cuts)))
        level = level * jnp.repeat(heights, dims[position] // shards_of).reshape([-1 if axis == position else 1 for axis in range(len(dims))])
    return level


def normal_values(own_key, dims, spread, most, cuts=(), held_as=jnp.bfloat16):
    array = spread * jax.random.normal(own_key, dims, jnp.float32)
    if cuts:
        array = array * block_scale(own_key, dims, cuts, -0.22, 0.18)
    return jnp.clip(array, -most, most).astype(held_as)


def setup_inputs(seed: int = 0) -> dict:
    keys = jax.random.split(jax.random.key(seed), 15)
    return {
        "inputs": draw_inputs(jax.random.fold_in(keys[14], 71), 0),
        "qkv_weight": draw_qkv_weight(jax.random.fold_in(keys[14], 71), 0),
        "qkv_bias": normal_values(keys[2], (3 * D,), 0.5, 3.0, ((0, 4),)),
        "out_weight": normal_values(keys[3], (D, D), (max(1, D // 8)) ** -0.5, 0.625, ((0, 4),)),
        "out_bias": normal_values(keys[4], (D,), 0.5, 3.0, ((0, 4),)),
        "up_weight": normal_values(keys[5], (D, FF), D ** -0.5, 0.21875, ((0, 4),)),
        "up_bias": normal_values(keys[6], (FF,), 0.5, 3.0, ((0, 4),)),
        "down_weight": normal_values(keys[7], (FF, D), FF ** -0.5, 0.109375, ((0, 4),)),
        "down_bias": normal_values(keys[8], (D,), 0.5, 3.0, ((0, 4),)),
        "attn_gain": jnp.clip(1.0 + 0.1 * jax.random.normal(keys[9], (D,), jnp.float32), 0.5, 1.5).astype(jnp.bfloat16),
        "attn_shift": normal_values(keys[10], (D,), 0.3, 2.0, ((0, 4),)),
        "mlp_gain": jnp.clip(1.0 + 0.1 * jax.random.normal(keys[11], (D,), jnp.float32), 0.5, 1.5).astype(jnp.bfloat16),
        "mlp_shift": normal_values(keys[12], (D,), 0.3, 2.0, ((0, 4),)),
        "cotangent": normal_values(keys[13], (SEQS, SEQ, D), 1.0, 6.0, ((0, 8), (1, 4)), jnp.float32),
    }


eps = 1e-05

def layer_norm(values):
    centered = values - lax.optimization_barrier(jnp.mean(values, axis=-1, keepdims=True))
    variance = lax.optimization_barrier(jnp.mean(centered * centered, axis=-1, keepdims=True))
    inverse = lax.rsqrt(variance + eps)
    return (centered * inverse, inverse)

def gelu_parts(preact):
    normal_cdf = 0.5 * (1.0 + jax.scipy.special.erf(preact * 0.7071067811865476))
    density = jnp.exp(-0.5 * preact * preact) * 0.3989422804014327
    return (preact * normal_cdf, normal_cdf + preact * density)

def angle_tables(positions):
    half_rot = ROT // 2
    frequency = 10000.0 ** (-jnp.arange(half_rot, dtype=jnp.float32) * (2.0 / ROT))
    angles = positions.astype(jnp.float32)[:, None] * frequency[None, :]
    return (jnp.cos(angles)[:, None, :], jnp.sin(angles)[:, None, :])

def rotate(tensor, cos_table, sin_table):
    half_rot = ROT // 2
    lower_part = tensor[..., :half_rot]
    upper_part = tensor[..., half_rot:ROT]
    return jnp.concatenate([lower_part * cos_table - upper_part * sin_table, upper_part * cos_table + lower_part * sin_table, tensor[..., ROT:]], axis=-1)

def unrotate(tensor, cos_table, sin_table):
    half_rot = ROT // 2
    lower_part = tensor[..., :half_rot]
    upper_part = tensor[..., half_rot:ROT]
    return jnp.concatenate([lower_part * cos_table + upper_part * sin_table, upper_part * cos_table - lower_part * sin_table, tensor[..., ROT:]], axis=-1)

def widen(tensor):
    return lax.optimization_barrier(tensor).astype(jnp.float32)

def reference(inputs, qkv_weight, qkv_bias, out_weight, out_bias, up_weight, up_bias, down_weight, down_bias, attn_gain, attn_shift, mlp_gain, mlp_shift, cotangent):
    positions = jnp.arange(SEQ, dtype=jnp.int32)
    cos_table, sin_table = angle_tables(positions)
    visible = positions[None, :] <= positions[:, None]
    score_scale = HD ** (-0.5)
    gain_attn = attn_gain.astype(jnp.float32)
    shift_attn = attn_shift.astype(jnp.float32)
    gain_mlp = mlp_gain.astype(jnp.float32)
    shift_mlp = mlp_shift.astype(jnp.float32)

    def one_sequence(carry, operands):
        sequence, grad_out = operands
        hidden_in = sequence.astype(jnp.float32)
        normed, inverse = layer_norm(hidden_in)
        attn_in = (normed * gain_attn + shift_attn).astype(jnp.bfloat16)
        mlp_in = (normed * gain_mlp + shift_mlp).astype(jnp.bfloat16)
        qkv = jnp.dot(attn_in, qkv_weight, preferred_element_type=jnp.float32) + qkv_bias.astype(jnp.float32)
        query_b = rotate(qkv[:, :D].reshape(SEQ, HEADS, HD), cos_table, sin_table).astype(jnp.bfloat16)
        keys_b = rotate(qkv[:, D:2 * D].reshape(SEQ, HEADS, HD), cos_table, sin_table).astype(jnp.bfloat16)
        values_b = qkv[:, 2 * D:].reshape(SEQ, HEADS, HD).astype(jnp.bfloat16)
        query_w = widen(query_b)
        keys_w = widen(keys_b)
        values_w = widen(values_b)
        scores = jnp.einsum('qhd,khd->hqk', query_w, keys_w) * score_scale
        scores = jnp.where(visible[None], scores, -jnp.inf)
        row_max = lax.optimization_barrier(jnp.max(scores, axis=-1, keepdims=True))
        log_total = row_max + jnp.log(lax.optimization_barrier(jnp.sum(jnp.exp(scores - row_max), axis=-1, keepdims=True)))
        attn_probs = jnp.exp(scores - log_total)
        probs_w = widen(attn_probs.astype(jnp.bfloat16))
        context = jnp.einsum('hqk,khd->qhd', probs_w, values_w).astype(jnp.bfloat16).reshape(SEQ, D)
        attn_out = jnp.dot(context, out_weight, preferred_element_type=jnp.float32) + out_bias.astype(jnp.float32)
        preact = jnp.dot(mlp_in, up_weight, preferred_element_type=jnp.float32) + up_bias.astype(jnp.float32)
        activation, slope = gelu_parts(preact)
        act_b = activation.astype(jnp.bfloat16)
        mlp_out = jnp.dot(act_b, down_weight, preferred_element_type=jnp.float32) + down_bias.astype(jnp.float32)
        block_out = hidden_in + attn_out + mlp_out
        grad_b = grad_out.astype(jnp.bfloat16)
        down_grad = jnp.dot(act_b.T, grad_b, preferred_element_type=jnp.float32)
        out_grad = jnp.dot(context.T, grad_b, preferred_element_type=jnp.float32)
        bias_sum = lax.optimization_barrier(jnp.sum(grad_out, axis=0))
        preact_grad = jnp.dot(grad_b, down_weight.T, preferred_element_type=jnp.float32) * slope
        up_bias_grad = lax.optimization_barrier(jnp.sum(preact_grad, axis=0))
        preact_b = preact_grad.astype(jnp.bfloat16)
        up_grad = jnp.dot(mlp_in.T, preact_b, preferred_element_type=jnp.float32)
        mlp_in_grad = jnp.dot(preact_b, up_weight.T, preferred_element_type=jnp.float32)
        context_grad = jnp.dot(grad_b, out_weight.T, preferred_element_type=jnp.float32).astype(jnp.bfloat16).reshape(SEQ, HEADS, HD)
        context_w = widen(context_grad)
        prob_grad = jnp.einsum('qhd,khd->hqk', context_w, values_w)
        row_dot = lax.optimization_barrier(jnp.sum(attn_probs * prob_grad, axis=-1, keepdims=True))
        score_grad = widen((attn_probs * (prob_grad - row_dot) * score_scale).astype(jnp.bfloat16))
        query_grad = jnp.einsum('hqk,khd->qhd', score_grad, keys_w)
        key_grad = jnp.einsum('hqk,qhd->khd', score_grad, query_w)
        value_grad = jnp.einsum('hqk,qhd->khd', probs_w, context_w)
        qkv_rows = jnp.concatenate([unrotate(query_grad, cos_table, sin_table).reshape(SEQ, D), unrotate(key_grad, cos_table, sin_table).reshape(SEQ, D), value_grad.reshape(SEQ, D)], axis=1)
        qkv_bias_grad = lax.optimization_barrier(jnp.sum(qkv_rows, axis=0))
        qkv_rows_b = qkv_rows.astype(jnp.bfloat16)
        qkv_grad = jnp.dot(attn_in.T, qkv_rows_b, preferred_element_type=jnp.float32)
        attn_in_grad = jnp.dot(qkv_rows_b, qkv_weight.T, preferred_element_type=jnp.float32)
        attn_gain_grad = lax.optimization_barrier(jnp.sum(attn_in_grad * normed, axis=0))
        attn_shift_grad = lax.optimization_barrier(jnp.sum(attn_in_grad, axis=0))
        mlp_gain_grad = lax.optimization_barrier(jnp.sum(mlp_in_grad * normed, axis=0))
        mlp_shift_grad = lax.optimization_barrier(jnp.sum(mlp_in_grad, axis=0))
        normed_grad = attn_in_grad * gain_attn + mlp_in_grad * gain_mlp
        input_grad = grad_out + inverse * (normed_grad - lax.optimization_barrier(jnp.mean(normed_grad, axis=-1, keepdims=True)) - normed * lax.optimization_barrier(jnp.mean(normed_grad * normed, axis=-1, keepdims=True)))
        pieces = (qkv_grad, qkv_bias_grad, out_grad, bias_sum, up_grad, up_bias_grad, down_grad, bias_sum, attn_gain_grad, attn_shift_grad, mlp_gain_grad, mlp_shift_grad)
        updated = tuple((summed + portion for summed, portion in zip(carry, pieces)))
        return (updated, (block_out, input_grad))
    shapes = ((D, 3 * D), (3 * D,), (D, D), (D,), (D, FF), (FF,), (FF, D), (D,), (D,), (D,), (D,), (D,))
    starting = tuple((jnp.zeros(shape_one, jnp.float32) for shape_one in shapes))
    totals, (block_outs, input_grads) = lax.scan(one_sequence, starting, (inputs, cotangent))
    return (block_outs, input_grads, totals[0], totals[1], totals[2], totals[3], totals[4], totals[5], totals[6], totals[7], totals[8], totals[9], totals[10], totals[11])
```

```python
import jax
import jax.numpy as jnp
from jax import lax
from jax.sharding import PartitionSpec as P

D = 768
HEADS = 12
HD = 64
ROT = 16


eps = 1e-05


def layer_norm(values):
    centered = values - jnp.mean(values, axis=-1, keepdims=True)
    variance = jnp.mean(centered * centered, axis=-1, keepdims=True)
    inverse = lax.rsqrt(variance + eps)
    return (centered * inverse, inverse)


def gelu_parts(preact):
    normal_cdf = 0.5 * (1.0 + jax.scipy.special.erf(preact * 0.7071067811865476))
    density = jnp.exp(-0.5 * preact * preact) * 0.3989422804014327
    return (preact * normal_cdf, normal_cdf + preact * density)


def angle_tables(positions):
    half_rot = ROT // 2
    frequency = 10000.0 ** (-jnp.arange(half_rot, dtype=jnp.float32) * (2.0 / ROT))
    angles = positions.astype(jnp.float32)[:, None] * frequency[None, :]
    return (jnp.cos(angles)[:, None, :], jnp.sin(angles)[:, None, :])


def rotate(tensor, cos_table, sin_table):
    half_rot = ROT // 2
    lower_part = tensor[..., :half_rot]
    upper_part = tensor[..., half_rot:ROT]
    return jnp.concatenate(
        [
            lower_part * cos_table - upper_part * sin_table,
            upper_part * cos_table + lower_part * sin_table,
            tensor[..., ROT:],
        ],
        axis=-1,
    )


def unrotate(tensor, cos_table, sin_table):
    half_rot = ROT // 2
    lower_part = tensor[..., :half_rot]
    upper_part = tensor[..., half_rot:ROT]
    return jnp.concatenate(
        [
            lower_part * cos_table + upper_part * sin_table,
            upper_part * cos_table - lower_part * sin_table,
            tensor[..., ROT:],
        ],
        axis=-1,
    )


def local_by_tokens(
    inputs,
    qkv_weight,
    qkv_bias,
    out_weight,
    out_bias,
    up_weight,
    up_bias,
    down_weight,
    down_bias,
    attn_gain,
    attn_shift,
    mlp_gain,
    mlp_shift,
    cotangent,
):
    tokens = inputs.shape[1]
    (
        full_qkv,
        full_qkv_bias,
        full_out,
        full_out_bias,
        full_up,
        full_up_bias,
        full_down,
        full_down_bias,
        gain_attn,
        shift_attn,
        gain_mlp,
        shift_mlp,
    ) = (
        lax.all_gather(qkv_weight, "grp", axis=0, tiled=True),
        lax.all_gather(qkv_bias, "grp", axis=0, tiled=True),
        lax.all_gather(out_weight, "grp", axis=0, tiled=True),
        lax.all_gather(out_bias, "grp", axis=0, tiled=True),
        lax.all_gather(up_weight, "grp", axis=0, tiled=True),
        lax.all_gather(up_bias, "grp", axis=0, tiled=True),
        lax.all_gather(down_weight, "grp", axis=0, tiled=True),
        lax.all_gather(down_bias, "grp", axis=0, tiled=True),
        lax.all_gather(attn_gain, "grp", axis=0, tiled=True),
        lax.all_gather(attn_shift, "grp", axis=0, tiled=True),
        lax.all_gather(mlp_gain, "grp", axis=0, tiled=True),
        lax.all_gather(mlp_shift, "grp", axis=0, tiled=True),
    )
    first_row = lax.axis_index("grp") * tokens
    positions = first_row + jnp.arange(tokens, dtype=jnp.int32)
    cos_table, sin_table = angle_tables(positions)
    score_scale = HD ** (-0.5)
    hidden_in = inputs[0].astype(jnp.float32)
    normed, inverse = layer_norm(hidden_in)
    attn_in = (normed * gain_attn.astype(jnp.float32) + shift_attn.astype(jnp.float32)).astype(
        jnp.bfloat16
    )
    mlp_in = (normed * gain_mlp.astype(jnp.float32) + shift_mlp.astype(jnp.float32)).astype(
        jnp.bfloat16
    )
    qkv = jnp.dot(attn_in, full_qkv, preferred_element_type=jnp.float32) + full_qkv_bias.astype(
        jnp.float32
    )
    query_b = rotate(qkv[:, :D].reshape(tokens, HEADS, HD), cos_table, sin_table).astype(
        jnp.bfloat16
    )
    keys_local = (
        rotate(qkv[:, D : 2 * D].reshape(tokens, HEADS, HD), cos_table, sin_table)
        .astype(jnp.bfloat16)
        .reshape(tokens, D)
    )
    values_local = qkv[:, 2 * D :].astype(jnp.bfloat16)
    keys_all, values_all = (
        lax.all_gather(keys_local, "grp", axis=0, tiled=True),
        lax.all_gather(values_local, "grp", axis=0, tiled=True),
    )
    length = keys_all.shape[0]
    visible = jnp.arange(length, dtype=jnp.int32)[None, :] <= positions[:, None]
    query_heads = jnp.transpose(query_b, (1, 0, 2))
    key_heads = jnp.transpose(keys_all.reshape(length, HEADS, HD), (1, 0, 2))
    value_heads = jnp.transpose(values_all.reshape(length, HEADS, HD), (1, 0, 2))

    def forward_head(operands):
        query_one, key_one, value_one = operands
        scores = jnp.dot(query_one, key_one.T, preferred_element_type=jnp.float32) * score_scale
        scores = jnp.where(visible, scores, -jnp.inf)
        row_max = jnp.max(scores, axis=-1, keepdims=True)
        log_total = row_max + jnp.log(jnp.sum(jnp.exp(scores - row_max), axis=-1, keepdims=True))
        probs_b = jnp.exp(scores - log_total).astype(jnp.bfloat16)
        context_one = jnp.dot(probs_b, value_one, preferred_element_type=jnp.float32).astype(
            jnp.bfloat16
        )
        return (context_one, log_total)

    context_heads, log_totals = lax.map(forward_head, (query_heads, key_heads, value_heads))
    context = jnp.transpose(context_heads, (1, 0, 2)).reshape(tokens, D)
    attn_out = jnp.dot(
        context, full_out, preferred_element_type=jnp.float32
    ) + full_out_bias.astype(jnp.float32)
    preact = jnp.dot(mlp_in, full_up, preferred_element_type=jnp.float32) + full_up_bias.astype(
        jnp.float32
    )
    activation, slope = gelu_parts(preact)
    act_b = activation.astype(jnp.bfloat16)
    mlp_out = jnp.dot(act_b, full_down, preferred_element_type=jnp.float32) + full_down_bias.astype(
        jnp.float32
    )
    block_out = hidden_in + attn_out + mlp_out
    back_qkv, back_out, back_up, back_down, back_gain_attn, back_gain_mlp = (
        lax.all_gather(qkv_weight, "grp", axis=0, tiled=True),
        lax.all_gather(out_weight, "grp", axis=0, tiled=True),
        lax.all_gather(up_weight, "grp", axis=0, tiled=True),
        lax.all_gather(down_weight, "grp", axis=0, tiled=True),
        lax.all_gather(attn_gain, "grp", axis=0, tiled=True),
        lax.all_gather(mlp_gain, "grp", axis=0, tiled=True),
    )
    grad_out = cotangent[0]
    grad_b = grad_out.astype(jnp.bfloat16)
    down_grad = jnp.dot(act_b.T, grad_b, preferred_element_type=jnp.float32)
    out_grad = jnp.dot(context.T, grad_b, preferred_element_type=jnp.float32)
    bias_sum = jnp.sum(grad_out, axis=0)
    preact_grad = jnp.dot(grad_b, back_down.T, preferred_element_type=jnp.float32) * slope
    up_bias_grad = jnp.sum(preact_grad, axis=0)
    preact_b = preact_grad.astype(jnp.bfloat16)
    up_grad = jnp.dot(mlp_in.T, preact_b, preferred_element_type=jnp.float32)
    mlp_in_grad = jnp.dot(preact_b, back_up.T, preferred_element_type=jnp.float32)
    context_grad = jnp.dot(grad_b, back_out.T, preferred_element_type=jnp.float32).astype(
        jnp.bfloat16
    )
    context_grad_heads = jnp.transpose(context_grad.reshape(tokens, HEADS, HD), (1, 0, 2))

    def backward_head(operands):
        query_one, key_one, value_one, grad_one, log_total = operands
        scores = jnp.dot(query_one, key_one.T, preferred_element_type=jnp.float32) * score_scale
        scores = jnp.where(visible, scores, -jnp.inf)
        attn_probs = jnp.exp(scores - log_total)
        probs_b = attn_probs.astype(jnp.bfloat16)
        prob_grad = jnp.dot(grad_one, value_one.T, preferred_element_type=jnp.float32)
        row_dot = jnp.sum(attn_probs * prob_grad, axis=-1, keepdims=True)
        score_grad = (attn_probs * (prob_grad - row_dot) * score_scale).astype(jnp.bfloat16)
        query_grad = jnp.dot(score_grad, key_one, preferred_element_type=jnp.float32)
        key_grad = jnp.dot(score_grad.T, query_one, preferred_element_type=jnp.float32)
        value_grad = jnp.dot(probs_b.T, grad_one, preferred_element_type=jnp.float32)
        return (query_grad, key_grad, value_grad)

    query_grads, key_grads, value_grads = lax.map(
        backward_head, (query_heads, key_heads, value_heads, context_grad_heads, log_totals)
    )
    key_full = jnp.transpose(key_grads, (1, 0, 2)).reshape(length, D)
    value_full = jnp.transpose(value_grads, (1, 0, 2)).reshape(length, D)
    key_mine, value_mine = (
        lax.psum_scatter(key_full, "grp", scatter_dimension=0, tiled=True),
        lax.psum_scatter(value_full, "grp", scatter_dimension=0, tiled=True),
    )
    query_rows = unrotate(jnp.transpose(query_grads, (1, 0, 2)), cos_table, sin_table).reshape(
        tokens, D
    )
    key_rows = unrotate(key_mine.reshape(tokens, HEADS, HD), cos_table, sin_table).reshape(
        tokens, D
    )
    qkv_rows = jnp.concatenate([query_rows, key_rows, value_mine], axis=1)
    qkv_bias_grad = jnp.sum(qkv_rows, axis=0)
    qkv_rows_b = qkv_rows.astype(jnp.bfloat16)
    qkv_grad = jnp.dot(attn_in.T, qkv_rows_b, preferred_element_type=jnp.float32)
    attn_in_grad = jnp.dot(qkv_rows_b, back_qkv.T, preferred_element_type=jnp.float32)
    attn_gain_grad = jnp.sum(attn_in_grad * normed, axis=0)
    attn_shift_grad = jnp.sum(attn_in_grad, axis=0)
    mlp_gain_grad = jnp.sum(mlp_in_grad * normed, axis=0)
    mlp_shift_grad = jnp.sum(mlp_in_grad, axis=0)
    normed_grad = attn_in_grad * back_gain_attn.astype(
        jnp.float32
    ) + mlp_in_grad * back_gain_mlp.astype(jnp.float32)
    input_grad = grad_out + inverse * (
        normed_grad
        - jnp.mean(normed_grad, axis=-1, keepdims=True)
        - normed * jnp.mean(normed_grad * normed, axis=-1, keepdims=True)
    )
    group_parts = (
        lax.psum_scatter(qkv_grad, "grp", scatter_dimension=0, tiled=True),
        lax.psum_scatter(qkv_bias_grad, "grp", scatter_dimension=0, tiled=True),
        lax.psum_scatter(out_grad, "grp", scatter_dimension=0, tiled=True),
        lax.psum_scatter(bias_sum, "grp", scatter_dimension=0, tiled=True),
        lax.psum_scatter(up_grad, "grp", scatter_dimension=0, tiled=True),
        lax.psum_scatter(up_bias_grad, "grp", scatter_dimension=0, tiled=True),
        lax.psum_scatter(down_grad, "grp", scatter_dimension=0, tiled=True),
        lax.psum_scatter(attn_gain_grad, "grp", scatter_dimension=0, tiled=True),
        lax.psum_scatter(attn_shift_grad, "grp", scatter_dimension=0, tiled=True),
        lax.psum_scatter(mlp_gain_grad, "grp", scatter_dimension=0, tiled=True),
        lax.psum_scatter(mlp_shift_grad, "grp", scatter_dimension=0, tiled=True),
    )
    (
        qkv_part,
        qkv_bias_part,
        out_part,
        bias_part,
        up_part,
        up_bias_part,
        down_part,
        gain_attn_part,
        shift_attn_part,
        gain_mlp_part,
        shift_mlp_part,
    ) = group_parts
    (
        qkv_total,
        qkv_bias_total,
        out_total,
        bias_total,
        up_total,
        up_bias_total,
        down_total,
        gain_attn_total,
        shift_attn_total,
        gain_mlp_total,
        shift_mlp_total,
    ) = lax.psum(
        (
            qkv_part,
            qkv_bias_part,
            out_part,
            bias_part,
            up_part,
            up_bias_part,
            down_part,
            gain_attn_part,
            shift_attn_part,
            gain_mlp_part,
            shift_mlp_part,
        ),
        "rep",
    )
    return (
        block_out[None],
        input_grad[None],
        qkv_total,
        qkv_bias_total,
        out_total,
        bias_total,
        up_total,
        up_bias_total,
        down_total,
        bias_total,
        gain_attn_total,
        shift_attn_total,
        gain_mlp_total,
        shift_mlp_total,
    )


def rotary_tables(length):
    half_rot = ROT // 2
    frequency = 10000.0 ** (-jnp.arange(half_rot, dtype=jnp.float32) * (2.0 / ROT))
    angles = jnp.arange(length, dtype=jnp.float32)[:, None] * frequency[None, :]
    return (jnp.cos(angles)[:, None, :], jnp.sin(angles)[:, None, :])


def gather(array):
    return lax.all_gather(array, "grp", axis=0, tiled=True)


def local_by_heads(
    inputs,
    qkv_weight,
    qkv_bias,
    out_weight,
    out_bias,
    up_weight,
    up_bias,
    down_weight,
    down_bias,
    attn_gain,
    attn_shift,
    mlp_gain,
    mlp_shift,
    cotangent,
):
    f32, bf16 = jnp.float32, jnp.bfloat16
    group = lax.axis_size("grp")
    me = lax.axis_index("grp")
    tokens = inputs.shape[1]
    length = group * tokens
    rows = D // group
    heads = HEADS // group
    width = heads * HD
    hidden = up_weight.shape[1] // group

    def dot(a, b):
        return jnp.dot(a, b, preferred_element_type=f32)

    grad_out = cotangent[0]
    x_all, grad_b = (gather(inputs[0]), gather(grad_out.astype(bf16)))
    qkv_parts = jnp.transpose(qkv_weight.reshape(rows, 3, group, width), (2, 0, 1, 3)).reshape(
        group, rows, 3 * width
    )
    up_parts = jnp.transpose(up_weight.reshape(rows, group, hidden), (1, 0, 2))
    w_in = lax.all_to_all(
        jnp.concatenate([qkv_parts, up_parts], axis=2), "grp", 0, 0, tiled=True
    ).reshape(D, 3 * width + hidden)
    w_qkv, w_up = w_in[:, : 3 * width], w_in[:, 3 * width :]
    small = gather(
        jnp.concatenate(
            [qkv_bias, out_bias, down_bias, attn_gain, attn_shift, mlp_gain, mlp_shift]
        )[None]
    ).astype(f32)
    nb = qkv_bias.shape[0]
    bias_qkv = small[:, :nb].reshape(3, group, width)
    bias_qkv = lax.dynamic_index_in_dim(bias_qkv, me, 1, keepdims=False).reshape(3 * width)
    vec = [small[:, nb + i * rows : nb + (i + 1) * rows].reshape(D) for i in range(6)]
    bias_out, bias_down, gain_attn, shift_attn, gain_mlp, shift_mlp = vec

    hidden_in = x_all.astype(f32)
    normed, inverse = layer_norm(hidden_in)
    attn_in = (normed * gain_attn + shift_attn).astype(bf16)
    mlp_in = (normed * gain_mlp + shift_mlp).astype(bf16)
    qkv = dot(attn_in, w_qkv) + bias_qkv
    cos_table, sin_table = rotary_tables(length)

    def split(t):
        return t.reshape(length, heads, HD)

    query = jnp.transpose(
        rotate(split(qkv[:, :width]), cos_table, sin_table).astype(bf16), (1, 0, 2)
    )
    keys = jnp.transpose(
        rotate(split(qkv[:, width : 2 * width]), cos_table, sin_table).astype(bf16), (1, 0, 2)
    )
    values = jnp.transpose(split(qkv[:, 2 * width :]).astype(bf16), (1, 0, 2))
    visible = (
        jnp.arange(length, dtype=jnp.int32)[None, :] <= jnp.arange(length, dtype=jnp.int32)[:, None]
    )
    scale = HD ** (-0.5)

    def bdot(eq, a, b):
        return jnp.einsum(eq, a, b, preferred_element_type=f32)

    scores = bdot("hqd,hkd->hqk", query, keys) * scale
    scores = jnp.where(visible[None], scores, -jnp.inf)
    row_max = jnp.max(scores, axis=-1, keepdims=True)
    log_total = row_max + jnp.log(jnp.sum(jnp.exp(scores - row_max), axis=-1, keepdims=True))
    attn_probs = jnp.exp(scores - log_total)
    probs_b = attn_probs.astype(bf16)
    context = jnp.transpose(bdot("hqk,hkd->qhd", probs_b, values).astype(bf16), (0, 1, 2)).reshape(
        length, width
    )
    preact = dot(mlp_in, w_up) + up_bias.astype(f32)
    activation, slope = gelu_parts(preact)
    act_b = activation.astype(bf16)
    out_part = dot(context, out_weight) + dot(act_b, down_weight)
    out_sum = lax.psum_scatter(out_part.astype(bf16), "grp", scatter_dimension=0, tiled=True)
    block_out = inputs[0].astype(f32) + (bias_out + bias_down) + out_sum.astype(f32)

    down_grad = dot(act_b.T, grad_b)
    out_grad = dot(context.T, grad_b)
    preact_grad = dot(grad_b, down_weight.T) * slope
    up_bias_grad = jnp.sum(preact_grad, axis=0)
    preact_b = preact_grad.astype(bf16)
    up_grad = dot(mlp_in.T, preact_b)
    mlp_in_grad = dot(preact_b, w_up.T)
    context_grad = jnp.transpose(split(dot(grad_b, out_weight.T).astype(bf16)), (1, 0, 2))
    prob_grad = bdot("hqd,hkd->hqk", context_grad, values)
    row_dot = jnp.sum(attn_probs * prob_grad, axis=-1, keepdims=True)
    score_grad = (attn_probs * (prob_grad - row_dot) * scale).astype(bf16)
    query_grad = bdot("hqk,hkd->qhd", score_grad, keys)
    key_grad = bdot("hqk,hqd->khd", score_grad, query)
    value_grad = bdot("hqk,hqd->khd", probs_b, context_grad)
    qkv_rows = jnp.concatenate(
        [
            unrotate(query_grad, cos_table, sin_table).reshape(length, width),
            unrotate(key_grad, cos_table, sin_table).reshape(length, width),
            value_grad.reshape(length, width),
        ],
        axis=1,
    )
    qkv_bias_grad = jnp.sum(qkv_rows, axis=0)
    qkv_rows_b = qkv_rows.astype(bf16)
    qkv_grad = dot(attn_in.T, qkv_rows_b)
    attn_in_grad = dot(qkv_rows_b, w_qkv.T)
    normed_part = attn_in_grad * gain_attn + mlp_in_grad * gain_mlp
    normed_grad = lax.psum_scatter(
        normed_part.astype(bf16), "grp", scatter_dimension=0, tiled=True
    ).astype(f32)
    my_normed, my_inverse = layer_norm(inputs[0].astype(f32))
    input_grad = grad_out + my_inverse * (
        normed_grad
        - jnp.mean(normed_grad, axis=-1, keepdims=True)
        - my_normed * jnp.mean(normed_grad * my_normed, axis=-1, keepdims=True)
    )

    one_hot = (jnp.arange(group) == me).astype(f32)
    vectors = jnp.concatenate(
        [
            (one_hot[None, :, None] * qkv_bias_grad.reshape(3, 1, width)).reshape(-1),
            (one_hot[:, None] * up_bias_grad[None]).reshape(-1),
            jnp.sum(grad_out, axis=0),
            jnp.sum(attn_in_grad * normed, axis=0),
            jnp.sum(attn_in_grad, axis=0),
            jnp.sum(mlp_in_grad * normed, axis=0),
            jnp.sum(mlp_in_grad, axis=0),
        ]
    )
    vectors = lax.psum(vectors, ("grp", "rep"))
    nu = up_bias.shape[0]
    offset = 0

    def take(size):
        nonlocal offset
        piece = lax.dynamic_slice_in_dim(vectors, offset + me * size, size)
        offset += group * size
        return piece

    qkv_bias_total = take(nb)
    up_bias_total = take(nu)
    bias_total, gain_attn_total, shift_attn_total, gain_mlp_total, shift_mlp_total = (
        take(rows),
        take(rows),
        take(rows),
        take(rows),
        take(rows),
    )
    back = lax.all_to_all(
        jnp.concatenate([qkv_grad, up_grad], axis=1).astype(bf16).reshape(group, rows, -1),
        "grp",
        0,
        0,
        tiled=True,
    )
    back, rest = lax.psum(
        (back, jnp.concatenate([down_grad, out_grad], axis=0).astype(bf16)), "rep"
    )
    back, rest = back.astype(f32), rest.astype(f32)
    qkv_total = jnp.transpose(
        back[:, :, : 3 * width].reshape(group, rows, 3, width), (1, 2, 0, 3)
    ).reshape(rows, 3 * D)
    up_total = jnp.transpose(back[:, :, 3 * width :], (1, 0, 2)).reshape(rows, group * hidden)
    return (
        block_out[None],
        input_grad[None],
        qkv_total,
        qkv_bias_total,
        rest[hidden:],
        bias_total,
        up_total,
        up_bias_total,
        rest[:hidden],
        bias_total,
        gain_attn_total,
        shift_attn_total,
        gain_mlp_total,
        shift_mlp_total,
    )


def solution(mesh):
    local = local_by_tokens if HEADS % mesh.shape["grp"] else local_by_heads
    placed = (
        P("rep", "grp", None),
        P("grp", None),
        P("grp"),
        P("grp", None),
        P("grp"),
        P("grp", None),
        P("grp"),
        P("grp", None),
        P("grp"),
        P("grp"),
        P("grp"),
        P("grp"),
        P("grp"),
        P("rep", "grp", None),
    )
    return jax.shard_map(
        local,
        mesh=mesh,
        in_specs=placed,
        out_specs=(
            P("rep", "grp", None),
            P("rep", "grp", None),
            P("grp", None),
            P("grp"),
            P("grp", None),
            P("grp"),
            P("grp", None),
            P("grp"),
            P("grp", None),
            P("grp"),
            P("grp"),
            P("grp"),
            P("grp"),
            P("grp"),
        ),
        check_vma=False,
    )
```

```python
import functools

import jax
import jax.numpy as jnp
from jax import lax
from jax.experimental import pallas as pl
from jax.experimental.pallas import tpu as pltpu
from jax.sharding import PartitionSpec as P

D = 768
HEADS = 12
HD = 64
ROT = 16


eps = 1e-05


def layer_norm(values):
    centered = values - jnp.mean(values, axis=-1, keepdims=True)
    variance = jnp.mean(centered * centered, axis=-1, keepdims=True)
    inverse = lax.rsqrt(variance + eps)
    return (centered * inverse, inverse)


def gelu_parts(preact):
    normal_cdf = 0.5 * (1.0 + jax.scipy.special.erf(preact * 0.7071067811865476))
    density = jnp.exp(-0.5 * preact * preact) * 0.3989422804014327
    return (preact * normal_cdf, normal_cdf + preact * density)


def angle_tables(positions):
    half_rot = ROT // 2
    frequency = 10000.0 ** (-jnp.arange(half_rot, dtype=jnp.float32) * (2.0 / ROT))
    angles = positions.astype(jnp.float32)[:, None] * frequency[None, :]
    return (jnp.cos(angles)[:, None, :], jnp.sin(angles)[:, None, :])


def rotate(tensor, cos_table, sin_table):
    half_rot = ROT // 2
    lower_part = tensor[..., :half_rot]
    upper_part = tensor[..., half_rot:ROT]
    return jnp.concatenate(
        [
            lower_part * cos_table - upper_part * sin_table,
            upper_part * cos_table + lower_part * sin_table,
            tensor[..., ROT:],
        ],
        axis=-1,
    )


def unrotate(tensor, cos_table, sin_table):
    half_rot = ROT // 2
    lower_part = tensor[..., :half_rot]
    upper_part = tensor[..., half_rot:ROT]
    return jnp.concatenate(
        [
            lower_part * cos_table + upper_part * sin_table,
            upper_part * cos_table - lower_part * sin_table,
            tensor[..., ROT:],
        ],
        axis=-1,
    )


def local_by_tokens(
    inputs,
    qkv_weight,
    qkv_bias,
    out_weight,
    out_bias,
    up_weight,
    up_bias,
    down_weight,
    down_bias,
    attn_gain,
    attn_shift,
    mlp_gain,
    mlp_shift,
    cotangent,
):
    tokens = inputs.shape[1]
    (
        full_qkv,
        full_qkv_bias,
        full_out,
        full_out_bias,
        full_up,
        full_up_bias,
        full_down,
        full_down_bias,
        gain_attn,
        shift_attn,
        gain_mlp,
        shift_mlp,
    ) = (
        lax.all_gather(qkv_weight, "grp", axis=0, tiled=True),
        lax.all_gather(qkv_bias, "grp", axis=0, tiled=True),
        lax.all_gather(out_weight, "grp", axis=0, tiled=True),
        lax.all_gather(out_bias, "grp", axis=0, tiled=True),
        lax.all_gather(up_weight, "grp", axis=0, tiled=True),
        lax.all_gather(up_bias, "grp", axis=0, tiled=True),
        lax.all_gather(down_weight, "grp", axis=0, tiled=True),
        lax.all_gather(down_bias, "grp", axis=0, tiled=True),
        lax.all_gather(attn_gain, "grp", axis=0, tiled=True),
        lax.all_gather(attn_shift, "grp", axis=0, tiled=True),
        lax.all_gather(mlp_gain, "grp", axis=0, tiled=True),
        lax.all_gather(mlp_shift, "grp", axis=0, tiled=True),
    )
    first_row = lax.axis_index("grp") * tokens
    positions = first_row + jnp.arange(tokens, dtype=jnp.int32)
    cos_table, sin_table = angle_tables(positions)
    score_scale = HD ** (-0.5)
    hidden_in = inputs[0].astype(jnp.float32)
    normed, inverse = layer_norm(hidden_in)
    attn_in = (normed * gain_attn.astype(jnp.float32) + shift_attn.astype(jnp.float32)).astype(
        jnp.bfloat16
    )
    mlp_in = (normed * gain_mlp.astype(jnp.float32) + shift_mlp.astype(jnp.float32)).astype(
        jnp.bfloat16
    )
    qkv = jnp.dot(attn_in, full_qkv, preferred_element_type=jnp.float32) + full_qkv_bias.astype(
        jnp.float32
    )
    query_b = rotate(qkv[:, :D].reshape(tokens, HEADS, HD), cos_table, sin_table).astype(
        jnp.bfloat16
    )
    keys_local = (
        rotate(qkv[:, D : 2 * D].reshape(tokens, HEADS, HD), cos_table, sin_table)
        .astype(jnp.bfloat16)
        .reshape(tokens, D)
    )
    values_local = qkv[:, 2 * D :].astype(jnp.bfloat16)
    keys_all, values_all = (
        lax.all_gather(keys_local, "grp", axis=0, tiled=True),
        lax.all_gather(values_local, "grp", axis=0, tiled=True),
    )
    length = keys_all.shape[0]
    visible = jnp.arange(length, dtype=jnp.int32)[None, :] <= positions[:, None]
    query_heads = jnp.transpose(query_b, (1, 0, 2))
    key_heads = jnp.transpose(keys_all.reshape(length, HEADS, HD), (1, 0, 2))
    value_heads = jnp.transpose(values_all.reshape(length, HEADS, HD), (1, 0, 2))

    def forward_head(operands):
        query_one, key_one, value_one = operands
        scores = jnp.dot(query_one, key_one.T, preferred_element_type=jnp.float32) * score_scale
        scores = jnp.where(visible, scores, -jnp.inf)
        row_max = jnp.max(scores, axis=-1, keepdims=True)
        log_total = row_max + jnp.log(jnp.sum(jnp.exp(scores - row_max), axis=-1, keepdims=True))
        probs_b = jnp.exp(scores - log_total).astype(jnp.bfloat16)
        context_one = jnp.dot(probs_b, value_one, preferred_element_type=jnp.float32).astype(
            jnp.bfloat16
        )
        return (context_one, log_total)

    context_heads, log_totals = lax.map(forward_head, (query_heads, key_heads, value_heads))
    context = jnp.transpose(context_heads, (1, 0, 2)).reshape(tokens, D)
    attn_out = jnp.dot(
        context, full_out, preferred_element_type=jnp.float32
    ) + full_out_bias.astype(jnp.float32)
    preact = jnp.dot(mlp_in, full_up, preferred_element_type=jnp.float32) + full_up_bias.astype(
        jnp.float32
    )
    activation, slope = gelu_parts(preact)
    act_b = activation.astype(jnp.bfloat16)
    mlp_out = jnp.dot(act_b, full_down, preferred_element_type=jnp.float32) + full_down_bias.astype(
        jnp.float32
    )
    block_out = hidden_in + attn_out + mlp_out
    back_qkv, back_out, back_up, back_down, back_gain_attn, back_gain_mlp = (
        lax.all_gather(qkv_weight, "grp", axis=0, tiled=True),
        lax.all_gather(out_weight, "grp", axis=0, tiled=True),
        lax.all_gather(up_weight, "grp", axis=0, tiled=True),
        lax.all_gather(down_weight, "grp", axis=0, tiled=True),
        lax.all_gather(attn_gain, "grp", axis=0, tiled=True),
        lax.all_gather(mlp_gain, "grp", axis=0, tiled=True),
    )
    grad_out = cotangent[0]
    grad_b = grad_out.astype(jnp.bfloat16)
    down_grad = jnp.dot(act_b.T, grad_b, preferred_element_type=jnp.float32)
    out_grad = jnp.dot(context.T, grad_b, preferred_element_type=jnp.float32)
    bias_sum = jnp.sum(grad_out, axis=0)
    preact_grad = jnp.dot(grad_b, back_down.T, preferred_element_type=jnp.float32) * slope
    up_bias_grad = jnp.sum(preact_grad, axis=0)
    preact_b = preact_grad.astype(jnp.bfloat16)
    up_grad = jnp.dot(mlp_in.T, preact_b, preferred_element_type=jnp.float32)
    mlp_in_grad = jnp.dot(preact_b, back_up.T, preferred_element_type=jnp.float32)
    context_grad = jnp.dot(grad_b, back_out.T, preferred_element_type=jnp.float32).astype(
        jnp.bfloat16
    )
    context_grad_heads = jnp.transpose(context_grad.reshape(tokens, HEADS, HD), (1, 0, 2))

    def backward_head(operands):
        query_one, key_one, value_one, grad_one, log_total = operands
        scores = jnp.dot(query_one, key_one.T, preferred_element_type=jnp.float32) * score_scale
        scores = jnp.where(visible, scores, -jnp.inf)
        attn_probs = jnp.exp(scores - log_total)
        probs_b = attn_probs.astype(jnp.bfloat16)
        prob_grad = jnp.dot(grad_one, value_one.T, preferred_element_type=jnp.float32)
        row_dot = jnp.sum(attn_probs * prob_grad, axis=-1, keepdims=True)
        score_grad = (attn_probs * (prob_grad - row_dot) * score_scale).astype(jnp.bfloat16)
        query_grad = jnp.dot(score_grad, key_one, preferred_element_type=jnp.float32)
        key_grad = jnp.dot(score_grad.T, query_one, preferred_element_type=jnp.float32)
        value_grad = jnp.dot(probs_b.T, grad_one, preferred_element_type=jnp.float32)
        return (query_grad, key_grad, value_grad)

    query_grads, key_grads, value_grads = lax.map(
        backward_head, (query_heads, key_heads, value_heads, context_grad_heads, log_totals)
    )
    key_full = jnp.transpose(key_grads, (1, 0, 2)).reshape(length, D)
    value_full = jnp.transpose(value_grads, (1, 0, 2)).reshape(length, D)
    key_mine, value_mine = (
        lax.psum_scatter(key_full, "grp", scatter_dimension=0, tiled=True),
        lax.psum_scatter(value_full, "grp", scatter_dimension=0, tiled=True),
    )
    query_rows = unrotate(jnp.transpose(query_grads, (1, 0, 2)), cos_table, sin_table).reshape(
        tokens, D
    )
    key_rows = unrotate(key_mine.reshape(tokens, HEADS, HD), cos_table, sin_table).reshape(
        tokens, D
    )
    qkv_rows = jnp.concatenate([query_rows, key_rows, value_mine], axis=1)
    qkv_bias_grad = jnp.sum(qkv_rows, axis=0)
    qkv_rows_b = qkv_rows.astype(jnp.bfloat16)
    qkv_grad = jnp.dot(attn_in.T, qkv_rows_b, preferred_element_type=jnp.float32)
    attn_in_grad = jnp.dot(qkv_rows_b, back_qkv.T, preferred_element_type=jnp.float32)
    attn_gain_grad = jnp.sum(attn_in_grad * normed, axis=0)
    attn_shift_grad = jnp.sum(attn_in_grad, axis=0)
    mlp_gain_grad = jnp.sum(mlp_in_grad * normed, axis=0)
    mlp_shift_grad = jnp.sum(mlp_in_grad, axis=0)
    normed_grad = attn_in_grad * back_gain_attn.astype(
        jnp.float32
    ) + mlp_in_grad * back_gain_mlp.astype(jnp.float32)
    input_grad = grad_out + inverse * (
        normed_grad
        - jnp.mean(normed_grad, axis=-1, keepdims=True)
        - normed * jnp.mean(normed_grad * normed, axis=-1, keepdims=True)
    )
    group_parts = (
        lax.psum_scatter(qkv_grad, "grp", scatter_dimension=0, tiled=True),
        lax.psum_scatter(qkv_bias_grad, "grp", scatter_dimension=0, tiled=True),
        lax.psum_scatter(out_grad, "grp", scatter_dimension=0, tiled=True),
        lax.psum_scatter(bias_sum, "grp", scatter_dimension=0, tiled=True),
        lax.psum_scatter(up_grad, "grp", scatter_dimension=0, tiled=True),
        lax.psum_scatter(up_bias_grad, "grp", scatter_dimension=0, tiled=True),
        lax.psum_scatter(down_grad, "grp", scatter_dimension=0, tiled=True),
        lax.psum_scatter(attn_gain_grad, "grp", scatter_dimension=0, tiled=True),
        lax.psum_scatter(attn_shift_grad, "grp", scatter_dimension=0, tiled=True),
        lax.psum_scatter(mlp_gain_grad, "grp", scatter_dimension=0, tiled=True),
        lax.psum_scatter(mlp_shift_grad, "grp", scatter_dimension=0, tiled=True),
    )
    (
        qkv_part,
        qkv_bias_part,
        out_part,
        bias_part,
        up_part,
        up_bias_part,
        down_part,
        gain_attn_part,
        shift_attn_part,
        gain_mlp_part,
        shift_mlp_part,
    ) = group_parts
    (
        qkv_total,
        qkv_bias_total,
        out_total,
        bias_total,
        up_total,
        up_bias_total,
        down_total,
        gain_attn_total,
        shift_attn_total,
        gain_mlp_total,
        shift_mlp_total,
    ) = lax.psum(
        (
            qkv_part,
            qkv_bias_part,
            out_part,
            bias_part,
            up_part,
            up_bias_part,
            down_part,
            gain_attn_part,
            shift_attn_part,
            gain_mlp_part,
            shift_mlp_part,
        ),
        "rep",
    )
    return (
        block_out[None],
        input_grad[None],
        qkv_total,
        qkv_bias_total,
        out_total,
        bias_total,
        up_total,
        up_bias_total,
        down_total,
        bias_total,
        gain_attn_total,
        shift_attn_total,
        gain_mlp_total,
        shift_mlp_total,
    )


CHUNKS = 4


def reduce_kernel(
    group,
    stages,
    grads,
    vectors,
    out,
    vector_out,
    pair_buf,
    hop_buf,
    send_buf,
    group_buf,
    total_buf,
    pair_s,
    pair_r,
    hop_s,
    hop_r,
    back_s,
    back_r,
    last_s,
    last_r,
    group_s,
    group_r,
    total_s,
    total_r,
):
    f32, bf16 = jnp.float32, jnp.bfloat16
    members = 2 * stages
    rep = lax.axis_index("rep")
    me = lax.axis_index("grp")
    core = lax.rem(rep, 2)
    stage = rep // 2
    partner = stage * 2 + (1 - core)

    barrier = pltpu.get_barrier_semaphore()
    for i in range(1, members):
        pl.semaphore_signal(
            barrier,
            inc=1,
            device_id={"rep": lax.rem(rep + i, members)},
            device_id_type=pl.DeviceIdType.MESH,
        )
    for i in range(1, group):
        pl.semaphore_signal(
            barrier,
            inc=1,
            device_id={"grp": lax.rem(me + i, group)},
            device_id_type=pl.DeviceIdType.MESH,
        )
    pl.semaphore_wait(barrier, members - 1 + group - 1)

    def copy(src, dst, send, recv, where):
        return pltpu.make_async_remote_copy(
            src_ref=src,
            dst_ref=dst,
            send_sem=send,
            recv_sem=recv,
            device_id=where,
            device_id_type=pl.DeviceIdType.MESH,
        )

    def place(d):
        return stage if d == 0 else stages - 1 - stage

    def at(d, step):
        shift = 2 * step if d == 0 else -2 * step
        return {"rep": lax.rem(rep + shift + members, members)}

    def pair(d, k):
        return copy(
            grads.at[1 - core, d, k],
            pair_buf.at[d, k],
            pair_s.at[d, k],
            pair_r.at[d, k],
            {"rep": partner},
        )

    def hop(d, k):
        return copy(
            send_buf.at[d, k], hop_buf.at[d, k], hop_s.at[d, k], hop_r.at[d, k], at(d, 1)
        )

    def back(d, k):
        return copy(
            out.at[core, d, k], out.at[core, d, k], back_s.at[d, k], back_r.at[d, k], at(d, -1)
        )

    def last(d, k, half):
        return copy(
            out.at[half, d, k],
            out.at[half, d, k],
            last_s.at[d, k],
            last_r.at[d, k],
            {"rep": partner},
        )

    for k in range(CHUNKS):
        for d in range(2):
            pair(d, k).start()

    def group_copy(i, slot):
        peer = lax.rem(me + i, group)
        return copy(
            vectors.at[peer], group_buf.at[slot], group_s.at[i - 1], group_r.at[slot], {"grp": peer}
        )

    def total_copy(i, slot):
        return copy(
            total_buf.at[rep],
            total_buf.at[slot],
            total_s.at[i - 1],
            total_r.at[slot],
            {"rep": lax.rem(rep + i, members)},
        )

    for i in range(1, group):
        group_copy(i, me).start()
    group_buf[me] = vectors[me]

    def reduce_chunk(d, k):
        position = place(d)
        pair(d, k).wait_recv()
        own = grads[core, d, k].astype(f32) + pair_buf[d, k].astype(f32)

        @pl.when(position == 0)
        def _():
            send_buf[d, k] = own.astype(bf16)
            hop(d, k).start()

        @pl.when(position > 0)
        def _():
            hop(d, k).wait_recv()
            total = (own + hop_buf[d, k].astype(f32)).astype(bf16)

            @pl.when(position < stages - 1)
            def _():
                send_buf[d, k] = total
                hop(d, k).start()

            @pl.when(position == stages - 1)
            def _():
                out[core, d, k] = total
                back(d, k).start()
                last(d, k, core).start()

    def return_chunk(d, k):
        position = place(d)

        @pl.when(position < stages - 1)
        def _():
            back(d, k).wait_recv()

            @pl.when(position > 0)
            def _():
                back(d, k).start()

            last(d, k, core).start()

    lag = stages - 1
    for t in range(CHUNKS + lag):
        if t < CHUNKS:
            for d in range(2):
                reduce_chunk(d, t)
        if t == 1:
            for i in range(1, group):
                group_copy(i, lax.rem(me + group - i, group)).wait_recv()
            chunk = group_buf[0]
            for i in range(1, group):
                chunk = chunk + group_buf[i]
            total_buf[rep] = chunk
            for i in range(1, members):
                total_copy(i, rep).start()
        if t >= lag:
            for d in range(2):
                return_chunk(d, t - lag)

    for i in range(1, members):
        total_copy(i, lax.rem(rep + members - i, members)).wait_recv()
    chunk = total_buf[0]
    for i in range(1, members):
        chunk = chunk + total_buf[i]
    vector_out[...] = chunk
    for i in range(1, group):
        group_copy(i, me).wait_send()
    for i in range(1, members):
        total_copy(i, rep).wait_send()
    for k in range(CHUNKS):
        for d in range(2):
            position = place(d)
            pair(d, k).wait_send()
            last(d, k, core).wait_send()
            last(d, k, 1 - core).wait_recv()

            @pl.when(position < stages - 1)
            def _():
                hop(d, k).wait_send()

            @pl.when(position > 0)
            def _():
                back(d, k).wait_send()


def reduce_over_rep(grads, vectors):
    group, members = lax.axis_size("grp"), lax.axis_size("rep")
    tile = grads.shape[3:]
    chunk = vectors.shape[1:]
    part = (2, CHUNKS) + tile
    dma = pltpu.SemaphoreType.DMA
    vmem = pl.BlockSpec(memory_space=pltpu.VMEM)
    return pl.pallas_call(
        functools.partial(reduce_kernel, group, members // 2),
        out_shape=(
            jax.ShapeDtypeStruct(grads.shape, grads.dtype),
            jax.ShapeDtypeStruct(chunk, vectors.dtype),
        ),
        in_specs=[vmem, vmem],
        out_specs=(vmem, vmem),
        scratch_shapes=[
            pltpu.VMEM(part, grads.dtype),
            pltpu.VMEM(part, grads.dtype),
            pltpu.VMEM(part, grads.dtype),
            pltpu.VMEM((group,) + chunk, vectors.dtype),
            pltpu.VMEM((members,) + chunk, vectors.dtype),
        ]
        + [dma((2, CHUNKS))] * 8
        + [dma((group - 1,)), dma((group,)), dma((members - 1,)), dma((members,))],
        compiler_params=pltpu.CompilerParams(collective_id=0, has_side_effects=True),
    )(grads, vectors)


def rotary_tables(length):
    half_rot = ROT // 2
    frequency = 10000.0 ** (-jnp.arange(half_rot, dtype=jnp.float32) * (2.0 / ROT))
    angles = jnp.arange(length, dtype=jnp.float32)[:, None] * frequency[None, :]
    return (jnp.cos(angles)[:, None, :], jnp.sin(angles)[:, None, :])


def gather(array):
    return lax.all_gather(array, "grp", axis=0, tiled=True)


def local_by_heads(
    inputs,
    qkv_weight,
    qkv_bias,
    out_weight,
    out_bias,
    up_weight,
    up_bias,
    down_weight,
    down_bias,
    attn_gain,
    attn_shift,
    mlp_gain,
    mlp_shift,
    cotangent,
):
    f32, bf16 = jnp.float32, jnp.bfloat16
    group = lax.axis_size("grp")
    me = lax.axis_index("grp")
    tokens = inputs.shape[1]
    length = group * tokens
    rows = D // group
    heads = HEADS // group
    width = heads * HD
    hidden = up_weight.shape[1] // group

    def dot(a, b):
        return jnp.dot(a, b, preferred_element_type=f32)

    grad_out = cotangent[0]
    small = jnp.concatenate(
        [qkv_bias, out_bias, down_bias, attn_gain, attn_shift, mlp_gain, mlp_shift]
    )
    extra = -(-small.shape[0] // (16 * D)) * 16
    small = jnp.pad(small, (0, extra * D - small.shape[0])).reshape(extra, D)
    packed = gather(jnp.concatenate([inputs[0], grad_out.astype(bf16), small], axis=0)[None])
    x_all = packed[:, :tokens].reshape(length, D)
    grad_b = packed[:, tokens : 2 * tokens].reshape(length, D)
    small = packed[:, 2 * tokens :].reshape(group, extra * D).astype(f32)
    qkv_parts = jnp.transpose(qkv_weight.reshape(rows, 3, group, width), (2, 0, 1, 3)).reshape(
        group, rows, 3 * width
    )
    up_parts = jnp.transpose(up_weight.reshape(rows, group, hidden), (1, 0, 2))
    w_in = lax.all_to_all(
        jnp.concatenate([qkv_parts, up_parts], axis=2), "grp", 0, 0, tiled=True
    ).reshape(D, 3 * width + hidden)
    w_qkv, w_up = w_in[:, : 3 * width], w_in[:, 3 * width :]
    nb = qkv_bias.shape[0]
    bias_qkv = small[:, :nb].reshape(3, group, width)
    bias_qkv = lax.dynamic_index_in_dim(bias_qkv, me, 1, keepdims=False).reshape(3 * width)
    vec = [small[:, nb + i * rows : nb + (i + 1) * rows].reshape(D) for i in range(6)]
    bias_out, bias_down, gain_attn, shift_attn, gain_mlp, shift_mlp = vec

    hidden_in = x_all.astype(f32)
    normed, inverse = layer_norm(hidden_in)
    attn_in = (normed * gain_attn + shift_attn).astype(bf16)
    mlp_in = (normed * gain_mlp + shift_mlp).astype(bf16)
    qkv = dot(attn_in, w_qkv) + bias_qkv
    cos_table, sin_table = rotary_tables(length)

    def split(t):
        return t.reshape(length, heads, HD)

    query = jnp.transpose(
        rotate(split(qkv[:, :width]), cos_table, sin_table).astype(bf16), (1, 0, 2)
    )
    keys = jnp.transpose(
        rotate(split(qkv[:, width : 2 * width]), cos_table, sin_table).astype(bf16), (1, 0, 2)
    )
    values = jnp.transpose(split(qkv[:, 2 * width :]).astype(bf16), (1, 0, 2))
    visible = (
        jnp.arange(length, dtype=jnp.int32)[None, :] <= jnp.arange(length, dtype=jnp.int32)[:, None]
    )
    scale = HD ** (-0.5)

    def bdot(eq, a, b):
        return jnp.einsum(eq, a, b, preferred_element_type=f32)

    scores = bdot("hqd,hkd->hqk", query, keys) * scale
    scores = jnp.where(visible[None], scores, -jnp.inf)
    row_max = jnp.max(scores, axis=-1, keepdims=True)
    log_total = row_max + jnp.log(jnp.sum(jnp.exp(scores - row_max), axis=-1, keepdims=True))
    attn_probs = jnp.exp(scores - log_total)
    probs_b = attn_probs.astype(bf16)
    context = jnp.transpose(bdot("hqk,hkd->qhd", probs_b, values).astype(bf16), (0, 1, 2)).reshape(
        length, width
    )
    preact = dot(mlp_in, w_up) + up_bias.astype(f32)
    activation, slope = gelu_parts(preact)
    act_b = activation.astype(bf16)
    out_part = dot(context, out_weight) + dot(act_b, down_weight)
    out_sum = lax.psum_scatter(out_part.astype(bf16), "grp", scatter_dimension=0, tiled=True)
    block_out = inputs[0].astype(f32) + (bias_out + bias_down) + out_sum.astype(f32)

    down_grad = dot(act_b.T, grad_b)
    out_grad = dot(context.T, grad_b)
    preact_grad = dot(grad_b, down_weight.T) * slope
    up_bias_grad = jnp.sum(preact_grad, axis=0)
    preact_b = preact_grad.astype(bf16)
    up_grad = dot(mlp_in.T, preact_b)
    mlp_in_grad = dot(preact_b, w_up.T)
    context_grad = jnp.transpose(split(dot(grad_b, out_weight.T).astype(bf16)), (1, 0, 2))
    prob_grad = bdot("hqd,hkd->hqk", context_grad, values)
    row_dot = jnp.sum(attn_probs * prob_grad, axis=-1, keepdims=True)
    score_grad = (attn_probs * (prob_grad - row_dot) * scale).astype(bf16)
    query_grad = bdot("hqk,hkd->qhd", score_grad, keys)
    key_grad = bdot("hqk,hqd->khd", score_grad, query)
    value_grad = bdot("hqk,hqd->khd", probs_b, context_grad)
    qkv_rows = jnp.concatenate(
        [
            unrotate(query_grad, cos_table, sin_table).reshape(length, width),
            unrotate(key_grad, cos_table, sin_table).reshape(length, width),
            value_grad.reshape(length, width),
        ],
        axis=1,
    )
    qkv_bias_grad = jnp.sum(qkv_rows, axis=0)
    qkv_rows_b = qkv_rows.astype(bf16)
    qkv_grad = dot(attn_in.T, qkv_rows_b)
    attn_in_grad = dot(qkv_rows_b, w_qkv.T)
    normed_part = attn_in_grad * gain_attn + mlp_in_grad * gain_mlp
    normed_grad = lax.psum_scatter(
        normed_part.astype(bf16), "grp", scatter_dimension=0, tiled=True
    ).astype(f32)
    my_normed, my_inverse = layer_norm(inputs[0].astype(f32))
    input_grad = grad_out + my_inverse * (
        normed_grad
        - jnp.mean(normed_grad, axis=-1, keepdims=True)
        - my_normed * jnp.mean(normed_grad * my_normed, axis=-1, keepdims=True)
    )

    mine = jnp.arange(group) == me
    nb, nu = qkv_bias.shape[0], up_bias.shape[0]
    vectors = jnp.concatenate(
        [
            jnp.where(mine[None, :, None], qkv_bias_grad.reshape(3, 1, width), 0.0).reshape(
                group, nb
            ),
            jnp.where(mine[:, None], up_bias_grad[None], 0.0),
            jnp.sum(grad_out, axis=0).reshape(group, rows),
            jnp.sum(attn_in_grad * normed, axis=0).reshape(group, rows),
            jnp.sum(attn_in_grad, axis=0).reshape(group, rows),
            jnp.sum(mlp_in_grad * normed, axis=0).reshape(group, rows),
            jnp.sum(mlp_in_grad, axis=0).reshape(group, rows),
        ],
        axis=1,
    )
    lines = -(-vectors.shape[1] // 1024) * 8
    vectors = jnp.pad(vectors, ((0, 0), (0, lines * 128 - vectors.shape[1])))
    vectors = vectors.reshape(group, lines, 128)
    back = lax.all_to_all(
        jnp.concatenate([qkv_grad, up_grad], axis=1).astype(bf16).reshape(group, rows, -1),
        "grp",
        0,
        0,
        tiled=True,
    )
    first = back.size // D
    grads = jnp.concatenate(
        [back.reshape(first, D), down_grad.astype(bf16), out_grad.astype(bf16)], axis=0
    )
    summed, vector_sum = reduce_over_rep(
        grads.reshape(2, 2, CHUNKS, grads.shape[0] // (4 * CHUNKS), D), vectors
    )
    summed = summed.reshape(grads.shape)
    back, rest = summed[:first].reshape(back.shape).astype(f32), summed[first:].astype(f32)
    vector_sum = vector_sum.reshape(-1)
    qkv_bias_total = vector_sum[:nb]
    up_bias_total = vector_sum[nb : nb + nu]
    bias_total, gain_attn_total, shift_attn_total, gain_mlp_total, shift_mlp_total = (
        vector_sum[nb + nu + i * rows : nb + nu + (i + 1) * rows] for i in range(5)
    )
    qkv_total = jnp.transpose(
        back[:, :, : 3 * width].reshape(group, rows, 3, width), (1, 2, 0, 3)
    ).reshape(rows, 3 * D)
    up_total = jnp.transpose(back[:, :, 3 * width :], (1, 0, 2)).reshape(rows, group * hidden)
    return (
        block_out[None],
        input_grad[None],
        qkv_total,
        qkv_bias_total,
        rest[hidden:],
        bias_total,
        up_total,
        up_bias_total,
        rest[:hidden],
        bias_total,
        gain_attn_total,
        shift_attn_total,
        gain_mlp_total,
        shift_mlp_total,
    )


def solution(mesh):
    group, members = mesh.shape["grp"], mesh.shape["rep"]
    by_heads = HEADS % group == 0 and members % 2 == 0 and members >= 4
    local = local_by_heads if by_heads else local_by_tokens
    placed = (
        P("rep", "grp", None),
        P("grp", None),
        P("grp"),
        P("grp", None),
        P("grp"),
        P("grp", None),
        P("grp"),
        P("grp", None),
        P("grp"),
        P("grp"),
        P("grp"),
        P("grp"),
        P("grp"),
        P("rep", "grp", None),
    )
    return jax.shard_map(
        local,
        mesh=mesh,
        in_specs=placed,
        out_specs=(
            P("rep", "grp", None),
            P("rep", "grp", None),
            P("grp", None),
            P("grp"),
            P("grp", None),
            P("grp"),
            P("grp", None),
            P("grp"),
            P("grp", None),
            P("grp"),
            P("grp"),
            P("grp"),
            P("grp"),
            P("grp"),
        ),
        check_vma=False,
    )
```

```python
import jax
import jax.numpy as jnp
from jax import lax
from jax.sharding import PartitionSpec as P

D = 768
HEADS = 12
HD = 64
ROT = 16


eps = 1e-05


def layer_norm(values):
    centered = values - jnp.mean(values, axis=-1, keepdims=True)
    variance = jnp.mean(centered * centered, axis=-1, keepdims=True)
    inverse = lax.rsqrt(variance + eps)
    return (centered * inverse, inverse)


def gelu_parts(preact):
    normal_cdf = 0.5 * (1.0 + jax.scipy.special.erf(preact * 0.7071067811865476))
    density = jnp.exp(-0.5 * preact * preact) * 0.3989422804014327
    return (preact * normal_cdf, normal_cdf + preact * density)


def angle_tables(positions):
    half_rot = ROT // 2
    frequency = 10000.0 ** (-jnp.arange(half_rot, dtype=jnp.float32) * (2.0 / ROT))
    angles = positions.astype(jnp.float32)[:, None] * frequency[None, :]
    return (jnp.cos(angles)[:, None, :], jnp.sin(angles)[:, None, :])


def rotate(tensor, cos_table, sin_table):
    half_rot = ROT // 2
    lower_part = tensor[..., :half_rot]
    upper_part = tensor[..., half_rot:ROT]
    return jnp.concatenate(
        [
            lower_part * cos_table - upper_part * sin_table,
            upper_part * cos_table + lower_part * sin_table,
            tensor[..., ROT:],
        ],
        axis=-1,
    )


def unrotate(tensor, cos_table, sin_table):
    half_rot = ROT // 2
    lower_part = tensor[..., :half_rot]
    upper_part = tensor[..., half_rot:ROT]
    return jnp.concatenate(
        [
            lower_part * cos_table + upper_part * sin_table,
            upper_part * cos_table - lower_part * sin_table,
            tensor[..., ROT:],
        ],
        axis=-1,
    )


def local_by_tokens(
    inputs,
    qkv_weight,
    qkv_bias,
    out_weight,
    out_bias,
    up_weight,
    up_bias,
    down_weight,
    down_bias,
    attn_gain,
    attn_shift,
    mlp_gain,
    mlp_shift,
    cotangent,
):
    tokens = inputs.shape[1]
    (
        full_qkv,
        full_qkv_bias,
        full_out,
        full_out_bias,
        full_up,
        full_up_bias,
        full_down,
        full_down_bias,
        gain_attn,
        shift_attn,
        gain_mlp,
        shift_mlp,
    ) = (
        lax.all_gather(qkv_weight, "grp", axis=0, tiled=True),
        lax.all_gather(qkv_bias, "grp", axis=0, tiled=True),
        lax.all_gather(out_weight, "grp", axis=0, tiled=True),
        lax.all_gather(out_bias, "grp", axis=0, tiled=True),
        lax.all_gather(up_weight, "grp", axis=0, tiled=True),
        lax.all_gather(up_bias, "grp", axis=0, tiled=True),
        lax.all_gather(down_weight, "grp", axis=0, tiled=True),
        lax.all_gather(down_bias, "grp", axis=0, tiled=True),
        lax.all_gather(attn_gain, "grp", axis=0, tiled=True),
        lax.all_gather(attn_shift, "grp", axis=0, tiled=True),
        lax.all_gather(mlp_gain, "grp", axis=0, tiled=True),
        lax.all_gather(mlp_shift, "grp", axis=0, tiled=True),
    )
    first_row = lax.axis_index("grp") * tokens
    positions = first_row + jnp.arange(tokens, dtype=jnp.int32)
    cos_table, sin_table = angle_tables(positions)
    score_scale = HD ** (-0.5)
    hidden_in = inputs[0].astype(jnp.float32)
    normed, inverse = layer_norm(hidden_in)
    attn_in = (normed * gain_attn.astype(jnp.float32) + shift_attn.astype(jnp.float32)).astype(
        jnp.bfloat16
    )
    mlp_in = (normed * gain_mlp.astype(jnp.float32) + shift_mlp.astype(jnp.float32)).astype(
        jnp.bfloat16
    )
    qkv = jnp.dot(attn_in, full_qkv, preferred_element_type=jnp.float32) + full_qkv_bias.astype(
        jnp.float32
    )
    query_b = rotate(qkv[:, :D].reshape(tokens, HEADS, HD), cos_table, sin_table).astype(
        jnp.bfloat16
    )
    keys_local = (
        rotate(qkv[:, D : 2 * D].reshape(tokens, HEADS, HD), cos_table, sin_table)
        .astype(jnp.bfloat16)
        .reshape(tokens, D)
    )
    values_local = qkv[:, 2 * D :].astype(jnp.bfloat16)
    keys_all, values_all = (
        lax.all_gather(keys_local, "grp", axis=0, tiled=True),
        lax.all_gather(values_local, "grp", axis=0, tiled=True),
    )
    length = keys_all.shape[0]
    visible = jnp.arange(length, dtype=jnp.int32)[None, :] <= positions[:, None]
    query_heads = jnp.transpose(query_b, (1, 0, 2))
    key_heads = jnp.transpose(keys_all.reshape(length, HEADS, HD), (1, 0, 2))
    value_heads = jnp.transpose(values_all.reshape(length, HEADS, HD), (1, 0, 2))

    def forward_head(operands):
        query_one, key_one, value_one = operands
        scores = jnp.dot(query_one, key_one.T, preferred_element_type=jnp.float32) * score_scale
        scores = jnp.where(visible, scores, -jnp.inf)
        row_max = jnp.max(scores, axis=-1, keepdims=True)
        log_total = row_max + jnp.log(jnp.sum(jnp.exp(scores - row_max), axis=-1, keepdims=True))
        probs_b = jnp.exp(scores - log_total).astype(jnp.bfloat16)
        context_one = jnp.dot(probs_b, value_one, preferred_element_type=jnp.float32).astype(
            jnp.bfloat16
        )
        return (context_one, log_total)

    context_heads, log_totals = lax.map(forward_head, (query_heads, key_heads, value_heads))
    context = jnp.transpose(context_heads, (1, 0, 2)).reshape(tokens, D)
    attn_out = jnp.dot(
        context, full_out, preferred_element_type=jnp.float32
    ) + full_out_bias.astype(jnp.float32)
    preact = jnp.dot(mlp_in, full_up, preferred_element_type=jnp.float32) + full_up_bias.astype(
        jnp.float32
    )
    activation, slope = gelu_parts(preact)
    act_b = activation.astype(jnp.bfloat16)
    mlp_out = jnp.dot(act_b, full_down, preferred_element_type=jnp.float32) + full_down_bias.astype(
        jnp.float32
    )
    block_out = hidden_in + attn_out + mlp_out
    back_qkv, back_out, back_up, back_down, back_gain_attn, back_gain_mlp = (
        lax.all_gather(qkv_weight, "grp", axis=0, tiled=True),
        lax.all_gather(out_weight, "grp", axis=0, tiled=True),
        lax.all_gather(up_weight, "grp", axis=0, tiled=True),
        lax.all_gather(down_weight, "grp", axis=0, tiled=True),
        lax.all_gather(attn_gain, "grp", axis=0, tiled=True),
        lax.all_gather(mlp_gain, "grp", axis=0, tiled=True),
    )
    grad_out = cotangent[0]
    grad_b = grad_out.astype(jnp.bfloat16)
    down_grad = jnp.dot(act_b.T, grad_b, preferred_element_type=jnp.float32)
    out_grad = jnp.dot(context.T, grad_b, preferred_element_type=jnp.float32)
    bias_sum = jnp.sum(grad_out, axis=0)
    preact_grad = jnp.dot(grad_b, back_down.T, preferred_element_type=jnp.float32) * slope
    up_bias_grad = jnp.sum(preact_grad, axis=0)
    preact_b = preact_grad.astype(jnp.bfloat16)
    up_grad = jnp.dot(mlp_in.T, preact_b, preferred_element_type=jnp.float32)
    mlp_in_grad = jnp.dot(preact_b, back_up.T, preferred_element_type=jnp.float32)
    context_grad = jnp.dot(grad_b, back_out.T, preferred_element_type=jnp.float32).astype(
        jnp.bfloat16
    )
    context_grad_heads = jnp.transpose(context_grad.reshape(tokens, HEADS, HD), (1, 0, 2))

    def backward_head(operands):
        query_one, key_one, value_one, grad_one, log_total = operands
        scores = jnp.dot(query_one, key_one.T, preferred_element_type=jnp.float32) * score_scale
        scores = jnp.where(visible, scores, -jnp.inf)
        attn_probs = jnp.exp(scores - log_total)
        probs_b = attn_probs.astype(jnp.bfloat16)
        prob_grad = jnp.dot(grad_one, value_one.T, preferred_element_type=jnp.float32)
        row_dot = jnp.sum(attn_probs * prob_grad, axis=-1, keepdims=True)
        score_grad = (attn_probs * (prob_grad - row_dot) * score_scale).astype(jnp.bfloat16)
        query_grad = jnp.dot(score_grad, key_one, preferred_element_type=jnp.float32)
        key_grad = jnp.dot(score_grad.T, query_one, preferred_element_type=jnp.float32)
        value_grad = jnp.dot(probs_b.T, grad_one, preferred_element_type=jnp.float32)
        return (query_grad, key_grad, value_grad)

    query_grads, key_grads, value_grads = lax.map(
        backward_head, (query_heads, key_heads, value_heads, context_grad_heads, log_totals)
    )
    key_full = jnp.transpose(key_grads, (1, 0, 2)).reshape(length, D)
    value_full = jnp.transpose(value_grads, (1, 0, 2)).reshape(length, D)
    key_mine, value_mine = (
        lax.psum_scatter(key_full, "grp", scatter_dimension=0, tiled=True),
        lax.psum_scatter(value_full, "grp", scatter_dimension=0, tiled=True),
    )
    query_rows = unrotate(jnp.transpose(query_grads, (1, 0, 2)), cos_table, sin_table).reshape(
        tokens, D
    )
    key_rows = unrotate(key_mine.reshape(tokens, HEADS, HD), cos_table, sin_table).reshape(
        tokens, D
    )
    qkv_rows = jnp.concatenate([query_rows, key_rows, value_mine], axis=1)
    qkv_bias_grad = jnp.sum(qkv_rows, axis=0)
    qkv_rows_b = qkv_rows.astype(jnp.bfloat16)
    qkv_grad = jnp.dot(attn_in.T, qkv_rows_b, preferred_element_type=jnp.float32)
    attn_in_grad = jnp.dot(qkv_rows_b, back_qkv.T, preferred_element_type=jnp.float32)
    attn_gain_grad = jnp.sum(attn_in_grad * normed, axis=0)
    attn_shift_grad = jnp.sum(attn_in_grad, axis=0)
    mlp_gain_grad = jnp.sum(mlp_in_grad * normed, axis=0)
    mlp_shift_grad = jnp.sum(mlp_in_grad, axis=0)
    normed_grad = attn_in_grad * back_gain_attn.astype(
        jnp.float32
    ) + mlp_in_grad * back_gain_mlp.astype(jnp.float32)
    input_grad = grad_out + inverse * (
        normed_grad
        - jnp.mean(normed_grad, axis=-1, keepdims=True)
        - normed * jnp.mean(normed_grad * normed, axis=-1, keepdims=True)
    )
    group_parts = (
        lax.psum_scatter(qkv_grad, "grp", scatter_dimension=0, tiled=True),
        lax.psum_scatter(qkv_bias_grad, "grp", scatter_dimension=0, tiled=True),
        lax.psum_scatter(out_grad, "grp", scatter_dimension=0, tiled=True),
        lax.psum_scatter(bias_sum, "grp", scatter_dimension=0, tiled=True),
        lax.psum_scatter(up_grad, "grp", scatter_dimension=0, tiled=True),
        lax.psum_scatter(up_bias_grad, "grp", scatter_dimension=0, tiled=True),
        lax.psum_scatter(down_grad, "grp", scatter_dimension=0, tiled=True),
        lax.psum_scatter(attn_gain_grad, "grp", scatter_dimension=0, tiled=True),
        lax.psum_scatter(attn_shift_grad, "grp", scatter_dimension=0, tiled=True),
        lax.psum_scatter(mlp_gain_grad, "grp", scatter_dimension=0, tiled=True),
        lax.psum_scatter(mlp_shift_grad, "grp", scatter_dimension=0, tiled=True),
    )
    (
        qkv_part,
        qkv_bias_part,
        out_part,
        bias_part,
        up_part,
        up_bias_part,
        down_part,
        gain_attn_part,
        shift_attn_part,
        gain_mlp_part,
        shift_mlp_part,
    ) = group_parts
    (
        qkv_total,
        qkv_bias_total,
        out_total,
        bias_total,
        up_total,
        up_bias_total,
        down_total,
        gain_attn_total,
        shift_attn_total,
        gain_mlp_total,
        shift_mlp_total,
    ) = lax.psum(
        (
            qkv_part,
            qkv_bias_part,
            out_part,
            bias_part,
            up_part,
            up_bias_part,
            down_part,
            gain_attn_part,
            shift_attn_part,
            gain_mlp_part,
            shift_mlp_part,
        ),
        "rep",
    )
    return (
        block_out[None],
        input_grad[None],
        qkv_total,
        qkv_bias_total,
        out_total,
        bias_total,
        up_total,
        up_bias_total,
        down_total,
        bias_total,
        gain_attn_total,
        shift_attn_total,
        gain_mlp_total,
        shift_mlp_total,
    )


def rotary_tables(length):
    half_rot = ROT // 2
    frequency = 10000.0 ** (-jnp.arange(half_rot, dtype=jnp.float32) * (2.0 / ROT))
    angles = jnp.arange(length, dtype=jnp.float32)[:, None] * frequency[None, :]
    return (jnp.cos(angles)[:, None, :], jnp.sin(angles)[:, None, :])


def gather(array):
    return lax.all_gather(array, "grp", axis=0, tiled=True)


def local_by_heads(
    inputs,
    qkv_weight,
    qkv_bias,
    out_weight,
    out_bias,
    up_weight,
    up_bias,
    down_weight,
    down_bias,
    attn_gain,
    attn_shift,
    mlp_gain,
    mlp_shift,
    cotangent,
):
    f32, bf16 = jnp.float32, jnp.bfloat16
    group = lax.axis_size("grp")
    me = lax.axis_index("grp")
    tokens = inputs.shape[1]
    length = group * tokens
    rows = D // group
    heads = HEADS // group
    width = heads * HD
    hidden = up_weight.shape[1] // group

    def dot(a, b):
        return jnp.dot(a, b, preferred_element_type=f32)

    grad_out = cotangent[0]
    small = jnp.concatenate(
        [qkv_bias, out_bias, down_bias, attn_gain, attn_shift, mlp_gain, mlp_shift]
    )
    extra = -(-small.shape[0] // (16 * D)) * 16
    small = jnp.pad(small, (0, extra * D - small.shape[0])).reshape(extra, D)
    packed = gather(jnp.concatenate([inputs[0], grad_out.astype(bf16), small], axis=0)[None])
    x_all = packed[:, :tokens].reshape(length, D)
    grad_b = packed[:, tokens : 2 * tokens].reshape(length, D)
    small = packed[:, 2 * tokens :].reshape(group, extra * D).astype(f32)
    qkv_parts = jnp.transpose(qkv_weight.reshape(rows, 3, group, width), (2, 0, 1, 3)).reshape(
        group, rows, 3 * width
    )
    up_parts = jnp.transpose(up_weight.reshape(rows, group, hidden), (1, 0, 2))
    w_in = lax.all_to_all(
        jnp.concatenate([qkv_parts, up_parts], axis=2), "grp", 0, 0, tiled=True
    ).reshape(D, 3 * width + hidden)
    w_qkv, w_up = w_in[:, : 3 * width], w_in[:, 3 * width :]
    nb = qkv_bias.shape[0]
    bias_qkv = small[:, :nb].reshape(3, group, width)
    bias_qkv = lax.dynamic_index_in_dim(bias_qkv, me, 1, keepdims=False).reshape(3 * width)
    vec = [small[:, nb + i * rows : nb + (i + 1) * rows].reshape(D) for i in range(6)]
    bias_out, bias_down, gain_attn, shift_attn, gain_mlp, shift_mlp = vec

    hidden_in = x_all.astype(f32)
    normed, inverse = layer_norm(hidden_in)
    attn_in = (normed * gain_attn + shift_attn).astype(bf16)
    mlp_in = (normed * gain_mlp + shift_mlp).astype(bf16)
    qkv = dot(attn_in, w_qkv) + bias_qkv
    cos_table, sin_table = rotary_tables(length)

    def split(t):
        return t.reshape(length, heads, HD)

    query = jnp.transpose(
        rotate(split(qkv[:, :width]), cos_table, sin_table).astype(bf16), (1, 0, 2)
    )
    keys = jnp.transpose(
        rotate(split(qkv[:, width : 2 * width]), cos_table, sin_table).astype(bf16), (1, 0, 2)
    )
    values = jnp.transpose(split(qkv[:, 2 * width :]).astype(bf16), (1, 0, 2))
    visible = (
        jnp.arange(length, dtype=jnp.int32)[None, :] <= jnp.arange(length, dtype=jnp.int32)[:, None]
    )
    scale = HD ** (-0.5)

    def bdot(eq, a, b):
        return jnp.einsum(eq, a, b, preferred_element_type=f32)

    scores = bdot("hqd,hkd->hqk", query, keys) * scale
    scores = jnp.where(visible[None], scores, -jnp.inf)
    row_max = jnp.max(scores, axis=-1, keepdims=True)
    log_total = row_max + jnp.log(jnp.sum(jnp.exp(scores - row_max), axis=-1, keepdims=True))
    attn_probs = jnp.exp(scores - log_total)
    probs_b = attn_probs.astype(bf16)
    context = jnp.transpose(bdot("hqk,hkd->qhd", probs_b, values).astype(bf16), (0, 1, 2)).reshape(
        length, width
    )
    preact = dot(mlp_in, w_up) + up_bias.astype(f32)
    activation, slope = gelu_parts(preact)
    act_b = activation.astype(bf16)
    out_part = dot(context, out_weight) + dot(act_b, down_weight)
    out_sum = lax.psum_scatter(out_part.astype(bf16), "grp", scatter_dimension=0, tiled=True)
    block_out = inputs[0].astype(f32) + (bias_out + bias_down) + out_sum.astype(f32)

    down_grad = dot(act_b.T, grad_b)
    out_grad = dot(context.T, grad_b)
    preact_grad = dot(grad_b, down_weight.T) * slope
    up_bias_grad = jnp.sum(preact_grad, axis=0)
    preact_b = preact_grad.astype(bf16)
    up_grad = dot(mlp_in.T, preact_b)
    mlp_in_grad = dot(preact_b, w_up.T)
    context_grad = jnp.transpose(split(dot(grad_b, out_weight.T).astype(bf16)), (1, 0, 2))
    prob_grad = bdot("hqd,hkd->hqk", context_grad, values)
    row_dot = jnp.sum(attn_probs * prob_grad, axis=-1, keepdims=True)
    score_grad = (attn_probs * (prob_grad - row_dot) * scale).astype(bf16)
    query_grad = bdot("hqk,hkd->qhd", score_grad, keys)
    key_grad = bdot("hqk,hqd->khd", score_grad, query)
    value_grad = bdot("hqk,hqd->khd", probs_b, context_grad)
    qkv_rows = jnp.concatenate(
        [
            unrotate(query_grad, cos_table, sin_table).reshape(length, width),
            unrotate(key_grad, cos_table, sin_table).reshape(length, width),
            value_grad.reshape(length, width),
        ],
        axis=1,
    )
    qkv_bias_grad = jnp.sum(qkv_rows, axis=0)
    qkv_rows_b = qkv_rows.astype(bf16)
    qkv_grad = dot(attn_in.T, qkv_rows_b)
    attn_in_grad = dot(qkv_rows_b, w_qkv.T)
    normed_part = attn_in_grad * gain_attn + mlp_in_grad * gain_mlp
    normed_grad = lax.psum_scatter(
        normed_part.astype(bf16), "grp", scatter_dimension=0, tiled=True
    ).astype(f32)
    my_normed, my_inverse = layer_norm(inputs[0].astype(f32))
    input_grad = grad_out + my_inverse * (
        normed_grad
        - jnp.mean(normed_grad, axis=-1, keepdims=True)
        - my_normed * jnp.mean(normed_grad * my_normed, axis=-1, keepdims=True)
    )

    one_hot = (jnp.arange(group) == me).astype(f32)
    vectors = jnp.concatenate(
        [
            (one_hot[None, :, None] * qkv_bias_grad.reshape(3, 1, width)).reshape(-1),
            (one_hot[:, None] * up_bias_grad[None]).reshape(-1),
            jnp.sum(grad_out, axis=0),
            jnp.sum(attn_in_grad * normed, axis=0),
            jnp.sum(attn_in_grad, axis=0),
            jnp.sum(mlp_in_grad * normed, axis=0),
            jnp.sum(mlp_in_grad, axis=0),
        ]
    )
    vectors = lax.psum(vectors, ("grp", "rep"))
    nu = up_bias.shape[0]
    offset = 0

    def take(size):
        nonlocal offset
        piece = lax.dynamic_slice_in_dim(vectors, offset + me * size, size)
        offset += group * size
        return piece

    qkv_bias_total = take(nb)
    up_bias_total = take(nu)
    bias_total, gain_attn_total, shift_attn_total, gain_mlp_total, shift_mlp_total = (
        take(rows),
        take(rows),
        take(rows),
        take(rows),
        take(rows),
    )
    back = lax.all_to_all(
        jnp.concatenate([qkv_grad, up_grad], axis=1).astype(bf16).reshape(group, rows, -1),
        "grp",
        0,
        0,
        tiled=True,
    )
    rest = lax.psum(jnp.concatenate([down_grad, out_grad], axis=0).astype(bf16), "rep")
    back, rest = lax.optimization_barrier((back, rest))
    back = lax.psum(back, "rep")
    back, rest = back.astype(f32), rest.astype(f32)
    qkv_total = jnp.transpose(
        back[:, :, : 3 * width].reshape(group, rows, 3, width), (1, 2, 0, 3)
    ).reshape(rows, 3 * D)
    up_total = jnp.transpose(back[:, :, 3 * width :], (1, 0, 2)).reshape(rows, group * hidden)
    return (
        block_out[None],
        input_grad[None],
        qkv_total,
        qkv_bias_total,
        rest[hidden:],
        bias_total,
        up_total,
        up_bias_total,
        rest[:hidden],
        bias_total,
        gain_attn_total,
        shift_attn_total,
        gain_mlp_total,
        shift_mlp_total,
    )


def solution(mesh):
    local = local_by_tokens if HEADS % mesh.shape["grp"] else local_by_heads
    placed = (
        P("rep", "grp", None),
        P("grp", None),
        P("grp"),
        P("grp", None),
        P("grp"),
        P("grp", None),
        P("grp"),
        P("grp", None),
        P("grp"),
        P("grp"),
        P("grp"),
        P("grp"),
        P("grp"),
        P("rep", "grp", None),
    )
    return jax.shard_map(
        local,
        mesh=mesh,
        in_specs=placed,
        out_specs=(
            P("rep", "grp", None),
            P("rep", "grp", None),
            P("grp", None),
            P("grp"),
            P("grp", None),
            P("grp"),
            P("grp", None),
            P("grp"),
            P("grp", None),
            P("grp"),
            P("grp"),
            P("grp"),
            P("grp"),
            P("grp"),
        ),
        check_vma=False,
    )
```
